768 devices in a mesh: node: 16 (over y, x_lo), feat: 48 (over z, x_hi, core).
Axes of the slice: x: 4 (x_hi: 2, x_lo: 2; x = x_hi * 2 + x_lo), y: 8, z: 12, core: 2. Of those that a mesh axis runs over, the one named last changes fastest.
Arguments:
- feats: bfloat16 [98304, 256], P(('node', 'feat')), may hold values from -6 to 6
- tile_values: bfloat16 [768, 144, 128, 128], P('node', 'feat'), may hold values from 0.049804688 to 1
- source_group: int32 [768, 144], P('node', 'feat'), may hold values from 0 to 15
- live_slots: int32 [768, 48], P('node', 'feat'), may hold values from 1 to 3, as said below
- proj_weight: bfloat16 [256, 256], replicated, may hold values from -0.375 to 0.375
- proj_bias: float32 [256], replicated, may hold values from -3 to 3
Outputs:
- updated: bfloat16 [98304, 256], P(('node', 'feat'))
The draws below stay inside these ranges and needn't reach their ends.
Inputs may be any that keep to these rules, and one draw needn't show every extreme that they name: `live_slots`: some tile row has all 3 slots live in some column block; slots at or past the count are not part of A.
All inputs are finite; a program needn't handle non-finite values.
Results may differ from the reference program's by a relative error of at most 0.0028.
Values may be sent and summed in bfloat16 or wider, within the bound.
A program may use at most 32 MiB of HBM per device.

```python
import math
import jax
import jax.numpy as jnp
import numpy as np
from jax import lax

FEATURES = 256
TILE = 128
SLOTS = 3
NODE_BLOCKS = 16
COLBLOCKS = 48
GROUPS = 768
NODES = 98304


def draw_live_slots(key, part):
    column_index = jnp.arange(COLBLOCKS, dtype=jnp.int32)[None, :]
    spread_last = max(COLBLOCKS - 1, 1)
    ceiling = 1 + (SLOTS - 1) * column_index // spread_last
    raw_draw = jax.random.randint(key, (GROUPS, COLBLOCKS), 0, 1 << 20, dtype=jnp.int32)
    drawn = 1 + raw_draw % ceiling
    leading = jnp.arange(GROUPS, dtype=jnp.int32)[:, None] % COLBLOCKS == 0
    return jnp.where(leading, ceiling, drawn).astype(jnp.int32)


def plant(entries, rng, smallest, largest):
    longest = entries.shape.index(max(entries.shape))
    spots = []
    for shift in (0, 1):
        where = [jax.random.randint(jax.random.fold_in(rng, axis), (), 0, length) for axis, length in enumerate(entries.shape)]
        where[longest] = (where[longest] + shift) % entries.shape[longest]
        spots.append(tuple(where))
    return entries.at[spots[0]].set(smallest).at[spots[1]].set(largest)


def shard_levels(rng, dims, split, low, high):
    def one(position, blocks):
        steps = jax.random.uniform(jax.random.fold_in(jax.random.fold_in(rng, 6), position), (blocks,), jnp.float32, low / len(split), high / len(split))
        return jnp.repeat(jnp.exp(steps), dims[position] // blocks).reshape((-1,) + (1,) * (len(dims) - position - 1))

    factor_of = one(*split[0])
    for cut in split[1:]:
        factor_of = factor_of * one(*cut)
    return factor_of


def rank_bounds(number_of, slope):
    loads = [(1 << 20) // math.isqrt(rank ** slope) + 1 for rank in range(1, number_of + 1)]
    width = 1 + sum(loads) // (1 << 30)
    return np.cumsum(np.array([max(1, weight // width) for weight in loads]))


def skewed_ids(stream_key, extent, amount, lean):
    table = rank_bounds(amount, lean)
    pick = jax.random.randint(jax.random.fold_in(stream_key, 1), extent, 0, int(table[amount - 1]))
    rank = jnp.searchsorted(jnp.asarray(table, jnp.int32), pick, side="right")
    return jax.random.permutation(jax.random.fold_in(stream_key, 2), amount)[rank].astype(jnp.int32)


def normal_values(key, shape, width, reach, split=(), held_as=jnp.bfloat16):
    array = width * jax.random.normal(key, shape, jnp.float32)
    if split:
        array = array * shard_levels(key, shape, split, -0.22, 0.18)
    return jnp.clip(array, -reach, reach).astype(held_as)


def setup_inputs(seed: int = 0) -> dict:
    key_of = jax.random.split(jax.random.key(seed), 7)
    return {
        "feats": normal_values(key_of[0], (NODES, FEATURES), 1.0, 6.0, ((0, 768),)),
        "tile_values": jnp.clip(0.049804688 + 0.9501953 * jax.random.uniform(key_of[1], (GROUPS, COLBLOCKS * SLOTS, TILE, TILE), jnp.float32) ** shard_levels(key_of[1], (GROUPS, COLBLOCKS * SLOTS, TILE, TILE), ((0, 16), (1, 48)), -0.2, 0.2), 0.049804688, 1.0).astype(jnp.bfloat16),
        "source_group": plant(skewed_ids(key_of[2], (GROUPS, COLBLOCKS * SLOTS), NODE_BLOCKS, 2), jax.random.fold_in(key_of[2], 3), 0, NODE_BLOCKS - 1).astype(jnp.int32),
        "live_slots": draw_live_slots(jax.random.fold_in(key_of[6], 71), 0),
        "proj_weight": normal_values(key_of[4], (FEATURES, FEATURES), FEATURES ** -0.5, 0.375),
        "proj_bias": normal_values(key_of[5], (FEATURES,), 0.5, 3.0, (), jnp.float32),
    }


def reference(feats, tile_values, source_group, live_slots, proj_weight, proj_bias):
    source_rows = feats.reshape(GROUPS, TILE, FEATURES)
    column_of = jnp.arange(COLBLOCKS * SLOTS, dtype=jnp.int32) // SLOTS
    slot_of = jnp.arange(COLBLOCKS * SLOTS, dtype=jnp.int32) % SLOTS

    def one_group(group_args):
        tiles, sources, live_row = group_args
        keep_slot = slot_of < live_row[column_of]
        adjacency = tiles.astype(jnp.float32)
        adjacency = jnp.where(keep_slot[:, None, None], adjacency, jnp.zeros_like(adjacency))
        gathered = source_rows[(sources * COLBLOCKS + column_of).astype(jnp.int32)].astype(jnp.float32)
        aggregate = jnp.einsum('sab,sbf->af', adjacency, gathered)
        degree_sum = 1.0 + lax.optimization_barrier(jnp.sum(adjacency, axis=(0, 2)))
        return (aggregate, degree_sum)
    aggregate, degree_sum = lax.map(one_group, (tile_values, source_group, live_slots))
    aggregate = aggregate.reshape(NODES, FEATURES)
    degree_sum = degree_sum.reshape(NODES)
    own_rows = feats.astype(jnp.float32)
    normed = ((aggregate + own_rows) * lax.rsqrt(degree_sum)[:, None]).astype(jnp.bfloat16)
    hidden = jnp.dot(normed, proj_weight, preferred_element_type=jnp.float32) + proj_bias.astype(jnp.float32)
    return (own_rows + jax.nn.relu(hidden)).astype(jnp.bfloat16)
```

```python
import jax
import jax.numpy as jnp
from jax import lax
from jax.experimental import pallas as pl
from jax.experimental.pallas import tpu as pltpu
from jax.sharding import PartitionSpec as P

SLOTS = 3
MESH = pl.DeviceIdType.MESH
F32 = jnp.float32
BF16 = jnp.bfloat16


def make_kernel(ny, nz):
    nodes = 2 * ny
    feats_n = 4 * nz
    half = nz // 2
    yhalf = ny // 2
    last = nz - 1

    def kernel(feats, tiles_hbm, src, live, weight, bias, out,
               tiles, fbuf, own, psend, precv, rsend, rrecv, xsend, xrecv,
               dmat, dpair, dsend, drecv, dxsend, dxrecv,
               tsem, ag_s, ag_r, p_s, p_r, r_s, r_r, x_s, x_r,
               dp_s, dp_r, dr_s, dr_r, dx_s, dx_r):
        n = lax.axis_index("node")
        f = lax.axis_index("feat")
        z = f // 4
        h = (f // 2) % 2
        c = f % 2
        n_x = n + 1 - 2 * (n % 2)
        n_up = (n + 2) % nodes
        n_dn = (n + nodes - 2) % nodes
        f_core = f + 1 - 2 * c
        f_opp = f + 2 - 4 * h
        f_up = (f + 4) % feats_n
        f_dn = (f + feats_n - 4) % feats_n

        rows_n = tiles_hbm.shape[0]
        parts = tsem.shape[0]
        step_rows = rows_n // parts

        def tile_copy(i):
            sl = pl.ds(i * step_rows, step_rows)
            return pltpu.make_async_copy(tiles_hbm.at[sl], tiles.at[sl], tsem.at[i])

        for i in range(parts):
            tile_copy(i).start()

        barrier = pltpu.get_barrier_semaphore()
        for dev in (dict(node=n_x), dict(node=n_up), dict(node=n_dn)):
            pl.semaphore_signal(barrier, inc=1, device_id=dict(node=dev["node"], feat=f), device_id_type=MESH)
        for fd in (f_core, f_opp, f_up, f_dn):
            pl.semaphore_signal(barrier, inc=1, device_id=dict(node=n, feat=fd), device_id_type=MESH)
        pl.semaphore_wait(barrier, 7)

        def remote(s, d, ss, rs, node=None, feat=None):
            dev = dict(node=n if node is None else node, feat=f if feat is None else feat)
            return pltpu.make_async_remote_copy(
                src_ref=s, dst_ref=d, send_sem=ss, recv_sem=rs, device_id=dev, device_id_type=MESH)

        def ag(way, block, source=None):
            dest = (n_x, n_up, n_dn)[way]
            s = fbuf.at[block] if source is None else source
            return remote(s, fbuf.at[block], ag_s.at[way, block], ag_r.at[block], node=dest)

        ag(0, n, feats).start()
        ag(1, n, feats).start()
        ag(2, n, feats).start()

        fbuf[n] = feats[...]
        fbuf[nodes] = jnp.zeros_like(feats)

        for i in range(parts):
            tile_copy(i).wait()
        lane = lax.broadcasted_iota(jnp.int32, (128, 128), 1)

        def degree_row(r, d):
            total = jnp.zeros((128, 128), F32)
            count = live[r, 0]
            for s in range(SLOTS):
                on = jnp.where(count > s, 1.0, 0.0).astype(F32)
                total = total + tiles[r, s].astype(F32) * on
            rowsum = jnp.sum(total, axis=1, keepdims=True)
            return jnp.where(lane == 8 * (r // 4) + r % 4, rowsum, d)

        d = lax.fori_loop(0, rows_n, degree_row, jnp.zeros((128, 128), F32))
        dmat[...] = d.T.reshape(16, 8, 128)
        dpc = remote(dmat, dpair, dp_s, dp_r, feat=f_core)
        dpc.start()

        ag(0, n_x).wait_recv()
        ag(1, n_x).start()
        ag(2, n_x).start()
        for dist in range(1, yhalf + 1):
            for base, way, reach in ((n, 1, yhalf), (n, 2, yhalf - 1), (n_x, 1, yhalf - 1), (n_x, 2, yhalf)):
                if dist > reach:
                    continue
                if way == 1:
                    block = (base + nodes - 2 * dist) % nodes
                else:
                    block = (base + 2 * dist) % nodes
                ag(way, block).wait_recv()
                if dist + 1 <= reach:
                    ag(way, block).start()

        def compute(u, carry):
            off = jnp.where(u % 2 == 1, half - (u + 1) // 2, half + u // 2)
            zt = (z + off) % nz

            def product(ht, ct):
                r = 4 * zt + 2 * ht + ct
                count = live[r, 0]
                a = jnp.concatenate([tiles[r, s] for s in range(SLOTS)], axis=1)
                b = jnp.concatenate(
                    [fbuf[jnp.where(count > s, src[r, s], nodes)] for s in range(SLOTS)], axis=0)
                return jnp.dot(a, b, preferred_element_type=F32)

            for ht in range(2):
                psend[u, ht] = product(ht, 1 - c).astype(BF16)
            pair(u).start()
            for ht in range(2):
                own[u, ht] = product(ht, c)
            return carry

        def pair(u):
            return remote(psend.at[u], precv.at[u], p_s.at[u], p_r.at[u], feat=f_core)

        is_up = (True, False, True, False)
        col = (0, 1, 1, 0)

        def ring(s, k):
            return remote(rsend.at[s, k], rrecv.at[s, k], r_s.at[s, k], r_r.at[s, k],
                          feat=f_up if is_up[s] else f_dn)

        def dring(way, k):
            return remote(dsend.at[way, k], drecv.at[way, k], dr_s.at[way, k], dr_r.at[way, k],
                          feat=f_dn if way else f_up)

        def ring_step(k, streams, incoming, first):
            for s in streams:
                u = 0 if first else (2 * k - 1 if is_up[s] else 2 * k)
                cs = slice(col[s] * 128, col[s] * 128 + 128)
                if s in incoming:
                    ring(s, k - 1).wait_recv()
                for ht in range(2):
                    v = own[u, ht, :, cs] + precv[u, ht, :, cs].astype(F32)
                    if s in incoming:
                        v = v + rrecv[s, k - 1, ht].astype(F32)
                    rsend[s, k, ht] = v.astype(BF16)
                ring(s, k).start()

        def dstep(k, ways, incoming):
            for way in ways:
                zt = (z + half - k) % nz if way == 0 else (z + half + k) % nz
                v = dmat[zt]
                if way in incoming:
                    dring(way, k - 1).wait_recv()
                    v = v + drecv[way, k - 1]
                dsend[way, k] = v
                dring(way, k).start()

        lax.fori_loop(0, 3, compute, 0)
        dpc.wait()
        dmat[...] = dmat[...] + dpair[...]
        pair(0).wait_recv()
        ring_step(0, (0, 1), (), True)
        dstep(0, (0,), ())
        pair(1).wait_recv()
        pair(2).wait_recv()
        ring_step(1, (0, 1, 2, 3), (0, 1), False)
        dstep(1, (0, 1), (0,))
        lax.fori_loop(3, 5, compute, 0)

        def mid(k, carry):
            pair(2 * k - 1).wait_recv()
            pair(2 * k).wait_recv()
            ring_step(k, (0, 1, 2, 3), (0, 1, 2, 3), False)
            dstep(k, (0, 1), (0, 1))
            lax.fori_loop(2 * k + 1, jnp.minimum(2 * k + 3, nz), compute, 0)
            return carry

        lax.fori_loop(2, half, mid, 0)

        pair(last).wait_recv()
        e = half - 1

        def total(ht):
            left = own[last, ht, :, 0:128] + precv[last, ht, :, 0:128].astype(F32)
            left = left + rrecv[0, e, ht].astype(F32) + rrecv[3, e, ht].astype(F32)
            right = own[last, ht, :, 128:256] + precv[last, ht, :, 128:256].astype(F32)
            right = right + rrecv[1, e, ht].astype(F32) + rrecv[2, e, ht].astype(F32)
            return left, right

        dring(0, e).wait_recv()
        dring(1, e).wait_recv()
        dxsend[...] = dmat[z] + drecv[0, e] + drecv[1, e]
        dxc = remote(dxsend, dxrecv, dx_s, dx_r, feat=f_opp)
        dxc.start()
        for s in range(4):
            ring(s, e).wait_recv()
        left, right = total(1 - h)
        xsend[:, 0:128] = left.astype(BF16)
        xsend[:, 128:256] = right.astype(BF16)
        xc = remote(xsend, xrecv, x_s, x_r, feat=f_opp)
        xc.start()
        left, right = total(h)
        mine = feats[...].astype(F32)
        agg = jnp.concatenate([left, right], axis=1) + mine

        dxc.wait_recv()
        drow = dxsend[pl.ds(2 * h + c, 1), :] + dxrecv[pl.ds(2 * h + c, 1), :] + 1.0
        inv = lax.rsqrt(jnp.broadcast_to(drow, (128, 128)).T)
        inv = jnp.concatenate([inv, inv], axis=1)
        xc.wait_recv()
        normed = ((agg + xrecv[...].astype(F32)) * inv).astype(BF16)
        hidden = jnp.dot(normed, weight[...], preferred_element_type=F32) + bias[...]
        out[...] = (mine + jnp.maximum(hidden, 0.0)).astype(BF16)

        xc.wait_send()
        dxc.wait_send()
        ag(0, n, feats).wait_send()
        ag(1, n, feats).wait_send()
        ag(2, n, feats).wait_send()
        ag(1, n_x).wait_send()
        ag(2, n_x).wait_send()
        for dist in range(1, yhalf):
            for base, way, reach in ((n, 1, yhalf), (n, 2, yhalf - 1), (n_x, 1, yhalf - 1), (n_x, 2, yhalf)):
                if dist + 1 > reach:
                    continue
                if way == 1:
                    block = (base + nodes - 2 * dist) % nodes
                else:
                    block = (base + 2 * dist) % nodes
                ag(way, block).wait_send()

        def drain_pair(u, carry):
            pair(u).wait_send()
            return carry

        lax.fori_loop(0, nz, drain_pair, 0)

        def drain_ring(k, carry):
            for s in range(4):
                ring(s, k).wait_send()
            dring(0, k).wait_send()
            dring(1, k).wait_send()
            return carry

        ring(0, 0).wait_send()
        ring(1, 0).wait_send()
        dring(0, 0).wait_send()
        lax.fori_loop(1, half, drain_ring, 0)

    return kernel


def make_body(ny, nz):
    nodes = 2 * ny
    half = nz // 2
    dma = pltpu.SemaphoreType.DMA
    vmem = pl.BlockSpec(memory_space=pltpu.VMEM)
    smem = pl.BlockSpec(memory_space=pltpu.SMEM)

    def body(feats, tile_values, source_group, live_slots, proj_weight, proj_bias):
        rows_n = tile_values.shape[0]
        scratch = [
            pltpu.VMEM((rows_n, SLOTS, 128, 128), BF16),
            pltpu.VMEM((nodes + 1, 128, 256), BF16),
            pltpu.VMEM((nz, 2, 128, 256), F32),
            pltpu.VMEM((nz, 2, 128, 256), BF16),
            pltpu.VMEM((nz, 2, 128, 256), BF16),
            pltpu.VMEM((4, half, 2, 128, 128), BF16),
            pltpu.VMEM((4, half, 2, 128, 128), BF16),
            pltpu.VMEM((128, 256), BF16),
            pltpu.VMEM((128, 256), BF16),
            pltpu.VMEM((16, 8, 128), F32),
            pltpu.VMEM((16, 8, 128), F32),
            pltpu.VMEM((2, half, 8, 128), F32),
            pltpu.VMEM((2, half, 8, 128), F32),
            pltpu.VMEM((8, 128), F32),
            pltpu.VMEM((8, 128), F32),
            dma((6,)),
            dma((3, nodes)), dma((nodes,)),
            dma((nz,)), dma((nz,)),
            dma((4, half)), dma((4, half)),
            dma, dma,
            dma, dma,
            dma((2, half)), dma((2, half)),
            dma, dma,
        ]
        return pl.pallas_call(
            make_kernel(ny, nz),
            out_shape=jax.ShapeDtypeStruct(feats.shape, BF16),
            in_specs=[vmem, pl.BlockSpec(memory_space=pl.ANY), smem, smem, vmem, vmem],
            out_specs=vmem,
            scratch_shapes=scratch,
            compiler_params=pltpu.CompilerParams(
                collective_id=0, has_side_effects=True, vmem_limit_bytes=60 << 20),
            name="graph_layer",
        )(feats, tile_values, source_group, live_slots, proj_weight, proj_bias.reshape(1, -1))

    return body


def solution(mesh):
    placed = (
        P(("node", "feat"), None),
        P("node", "feat", None, None),
        P("node", "feat"),
        P("node", "feat"),
        P(),
        P(),
    )
    return jax.shard_map(
        make_body(mesh.shape["node"] // 2, mesh.shape["feat"] // 4),
        mesh=mesh, in_specs=placed, out_specs=P(("node", "feat"), None), check_vma=False,
    )
```

```python
import jax
import jax.numpy as jnp
from jax import lax
from jax.experimental import pallas as pl
from jax.experimental.pallas import tpu as pltpu
from jax.sharding import PartitionSpec as P

SLOTS = 3
MESH = pl.DeviceIdType.MESH
F32 = jnp.float32
BF16 = jnp.bfloat16


def make_kernel(ny, nz):
    nodes = 2 * ny
    feats_n = 4 * nz
    half = nz // 2
    yhalf = ny // 2
    last = nz - 1

    def kernel(feats, tiles_hbm, src, live, weight, bias, out,
               tiles, fbuf, own, psend, precv, rsend, rrecv, xsend, xrecv,
               dloc, dsend, drecv, dtot, dxrecv,
               tsem, own_s, ag_s, ag_r, p_s, p_r, r_s, r_r, x_s, x_r,
               dr_s, dr_r, dx_s, dx_r):
        n = lax.axis_index("node")
        f = lax.axis_index("feat")
        z = f // 4
        h = (f // 2) % 2
        c = f % 2
        n_x = n + 1 - 2 * (n % 2)
        n_up = (n + 2) % nodes
        n_dn = (n + nodes - 2) % nodes
        f_core = f + 1 - 2 * c
        f_opp = f + 2 - 4 * h
        f_up = (f + 4) % feats_n
        f_dn = (f + feats_n - 4) % feats_n

        rows_n = tiles_hbm.shape[0]
        parts = tsem.shape[0]
        step_rows = rows_n // parts

        def tile_copy(i):
            sl = pl.ds(i * step_rows, step_rows)
            return pltpu.make_async_copy(tiles_hbm.at[sl], tiles.at[sl], tsem.at[i])

        for i in range(parts):
            tile_copy(i).start()

        barrier = pltpu.get_barrier_semaphore()
        near = [(nd, f) for nd in (n_x, n_up, n_dn, (n_x + 2) % nodes, (n_x + nodes - 2) % nodes)]
        near += [(n, fd) for fd in (f_core, f_opp, f_opp + 1 - 2 * c, f_up, f_dn)]
        for nd, fd in near:
            pl.semaphore_signal(barrier, inc=1, device_id=dict(node=nd, feat=fd), device_id_type=MESH)
        pl.semaphore_wait(barrier, len(near))

        def remote(s, d, ss, rs, node=None, feat=None):
            dev = dict(node=n if node is None else node, feat=f if feat is None else feat)
            return pltpu.make_async_remote_copy(
                src_ref=s, dst_ref=d, send_sem=ss, recv_sem=rs, device_id=dev, device_id_type=MESH)

        def block_at(base, way, dist):
            return (base + nodes - 2 * dist) % nodes if way == 0 else (base + 2 * dist) % nodes

        def ag(way, block, q):
            ref = fbuf.at[block, pl.ds(64 * q, 64)]
            return remote(ref, ref, ag_s.at[block, q], ag_r.at[block, q], node=n_dn if way else n_up)

        def ag_own(i, q):
            dest = (n_up, n_dn, n_x, (n_x + 2) % nodes, (n_x + nodes - 2) % nodes)[i]
            return remote(feats.at[pl.ds(64 * q, 64)], fbuf.at[n, pl.ds(64 * q, 64)],
                          own_s.at[i, q], ag_r.at[n, q], node=dest)

        hops = []
        for dist in range(1, yhalf + 1):
            for side in range(2):
                for q in range(2):
                    for way in range(2):
                        reach = yhalf if way == q else yhalf - 1
                        if dist <= reach:
                            hops.append((side, way, q, dist, dist < reach))

        for i in (0, 1, 3, 4, 2):
            for q in range(2):
                ag_own(i, q).start()

        fbuf[n] = feats[...]
        fbuf[nodes] = jnp.zeros_like(feats)
        dloc[...] = jnp.zeros_like(dloc)

        for side, way, q, dist, onward in hops:
            block = block_at(n_x if side else n, way, dist)
            ag(way, block, q).wait_recv()
            if onward:
                ag(way, block, q).start()
        for q in range(2):
            ag(0, n_x, q).wait_recv()
        for i in range(parts):
            tile_copy(i).wait()

        slot_of = lax.broadcasted_iota(jnp.int32, (16, SLOTS * 128), 1) // 128

        def pair(u):
            return remote(psend.at[u], precv.at[u], p_s.at[u], p_r.at[u], feat=f_core)

        def group(u, j):
            off = jnp.where(u % 2 == 1, half - (u + 1) // 2, half + u // 2)
            zt = (z + off) % nz
            ht = j % 2
            ct = 1 - c if j < 2 else c
            r = 4 * zt + 2 * ht + ct
            count = live[0, r]
            a = jnp.concatenate([tiles[r, s] for s in range(SLOTS)], axis=1)
            b = jnp.concatenate(
                [fbuf[jnp.where(count > s, src[s, r], nodes)] for s in range(SLOTS)], axis=0)
            on = jnp.where(slot_of < count, 1.0, 0.0).astype(BF16)
            got = jnp.dot(a, b, preferred_element_type=F32)
            rowsum = lax.dot_general(on, a, (((1,), (1,)), ((), ())), preferred_element_type=F32)
            dloc[u, pl.ds(2 * ht + ct, 1), :] = rowsum[0:1, :]
            if j < 2:
                psend[u, ht] = got.astype(BF16)
            else:
                own[u, ht] = got
            if j == 1:
                pair(u).start()

        streams = ((0, 0, 0), (1, 1, 0), (0, 0, 1), (1, 1, 1), (0, 1, 0), (1, 0, 0), (0, 1, 1), (1, 0, 1))
        far = streams[:4]

        def ring(s, k):
            w, q, ht = s
            return remote(rsend.at[w, q, ht, k], rrecv.at[w, q, ht, k], r_s.at[w, q, ht, k], r_r.at[w, q, ht, k],
                          feat=f_dn if w else f_up)

        def dring(w, k):
            return remote(dsend.at[w, k], drecv.at[w, k], dr_s.at[w, k], dr_r.at[w, k],
                          feat=f_dn if w else f_up)

        def ring_step(k, active, incoming, first, todo):
            todo = list(todo)
            for s in active:
                w, q, ht = s
                u = 0 if first else 2 * k - 1 + w
                cs = slice(q * 128, q * 128 + 128)
                if s in incoming:
                    ring(s, k - 1).wait_recv()
                v = own[u, ht, :, cs] + precv[u, ht, :, cs].astype(F32)
                if s in incoming:
                    v = v + rrecv[w, q, ht, k - 1].astype(F32)
                rsend[w, q, ht, k] = v.astype(BF16)
                ring(s, k).start()
                if todo:
                    group(*todo.pop(0))
            for t in todo:
                group(*t)

        def dstep(k, ways, incoming, first):
            for w in ways:
                v = dloc[0 if first else 2 * k - 1 + w]
                if w in incoming:
                    dring(w, k - 1).wait_recv()
                    v = v + drecv[w, k - 1]
                dsend[w, k] = v
                dring(w, k).start()

        def ahead(k):
            return [(u, j) for u in (2 * k + 2, 2 * k + 3) for j in range(4)]

        def begin(u, carry):
            for j in range(4):
                group(u, j)
            return carry

        lax.fori_loop(0, 2, begin, 0)
        pair(0).wait_recv()
        ring_step(0, far, (), True, ())
        dstep(0, (0,), (), True)
        lax.fori_loop(2, 4, begin, 0)
        pair(1).wait_recv()
        pair(2).wait_recv()
        ring_step(1, streams, far, False, ahead(1))
        dstep(1, (0, 1), (0,), False)

        def mid(k, carry):
            pair(2 * k - 1).wait_recv()
            pair(2 * k).wait_recv()
            ring_step(k, streams, streams, False, ahead(k))
            dstep(k, (0, 1), (0, 1), False)
            return carry

        lax.fori_loop(2, half - 1, mid, 0)
        e = half - 1
        pair(2 * e - 1).wait_recv()
        pair(2 * e).wait_recv()
        ring_step(e, streams, streams, False, ())
        dstep(e, (0, 1), (0, 1), False)
        pair(last).wait_recv()

        def total(ht, q):
            cs = slice(q * 128, q * 128 + 128)
            v = own[last, ht, :, cs] + precv[last, ht, :, cs].astype(F32)
            for w in range(2):
                ring((w, q, ht), e).wait_recv()
                v = v + rrecv[w, q, ht, e].astype(F32)
            return v

        def xc(q):
            return remote(xsend.at[q], xrecv.at[q], x_s.at[q], x_r.at[q], feat=f_opp)

        def dxc(i):
            return remote(dtot, dxrecv.at[i], dx_s.at[i], dx_r.at[i],
                          feat=(f_core, f_opp, f_opp + 1 - 2 * c)[i])

        for q in range(2):
            xsend[q] = total(1 - h, q).astype(BF16)
            xc(q).start()
        dring(0, e).wait_recv()
        dring(1, e).wait_recv()
        dtot[...] = dloc[last] + drecv[0, e] + drecv[1, e]
        for i in range(3):
            dxc(i).start()
        mine = feats[...].astype(F32)
        agg = jnp.concatenate([total(h, 0), total(h, 1)], axis=1) + mine
        row = pl.ds(2 * h + c, 1)
        drow = dtot[row, :] + 1.0
        for i in range(3):
            dxc(i).wait_recv()
            drow = drow + dxrecv[i, row, :]
        inv = lax.rsqrt(jnp.broadcast_to(drow, (128, 128)).T)
        inv = jnp.concatenate([inv, inv], axis=1)
        for q in range(2):
            xc(q).wait_recv()
        agg = agg + jnp.concatenate([xrecv[0], xrecv[1]], axis=1).astype(F32)
        normed = (agg * inv).astype(BF16)
        hidden = jnp.dot(normed, weight[...], preferred_element_type=F32) + bias[...]
        out[...] = (mine + jnp.maximum(hidden, 0.0)).astype(BF16)

        for q in range(2):
            xc(q).wait_send()
            for i in range(5):
                ag_own(i, q).wait_send()
        for i in range(3):
            dxc(i).wait_send()
        for side, way, q, dist, onward in hops:
            if onward:
                ag(way, block_at(n_x if side else n, way, dist), q).wait_send()

        def drain_pair(u, carry):
            pair(u).wait_send()
            return carry

        lax.fori_loop(0, nz, drain_pair, 0)

        def drain_ring(k, carry):
            for s in streams:
                ring(s, k).wait_send()
            dring(0, k).wait_send()
            dring(1, k).wait_send()
            return carry

        for s in far:
            ring(s, 0).wait_send()
        dring(0, 0).wait_send()
        lax.fori_loop(1, half, drain_ring, 0)

    return kernel


def make_body(ny, nz):
    nodes = 2 * ny
    half = nz // 2
    dma = pltpu.SemaphoreType.DMA
    vmem = pl.BlockSpec(memory_space=pltpu.VMEM)
    smem = pl.BlockSpec(memory_space=pltpu.SMEM)

    def body(feats, tile_values, source_group, live_slots, proj_weight, proj_bias):
        rows_n = tile_values.shape[0]
        scratch = [
            pltpu.VMEM((rows_n, SLOTS, 128, 128), BF16),
            pltpu.VMEM((nodes + 1, 128, 256), BF16),
            pltpu.VMEM((nz, 2, 128, 256), F32),
            pltpu.VMEM((nz, 2, 128, 256), BF16),
            pltpu.VMEM((nz, 2, 128, 256), BF16),
            pltpu.VMEM((2, 2, 2, half, 128, 128), BF16),
            pltpu.VMEM((2, 2, 2, half, 128, 128), BF16),
            pltpu.VMEM((2, 128, 128), BF16),
            pltpu.VMEM((2, 128, 128), BF16),
            pltpu.VMEM((nz, 8, 128), F32),
            pltpu.VMEM((2, half, 8, 128), F32),
            pltpu.VMEM((2, half, 8, 128), F32),
            pltpu.VMEM((8, 128), F32),
            pltpu.VMEM((3, 8, 128), F32),
            dma((6,)),
            dma((5, 2)), dma((nodes, 2)), dma((nodes, 2)),
            dma((nz,)), dma((nz,)),
            dma((2, 2, 2, half)), dma((2, 2, 2, half)),
            dma((2,)), dma((2,)),
            dma((2, half)), dma((2, half)),
            dma((3,)), dma((3,)),
        ]
        return pl.pallas_call(
            make_kernel(ny, nz),
            out_shape=jax.ShapeDtypeStruct(feats.shape, BF16),
            in_specs=[vmem, pl.BlockSpec(memory_space=pl.ANY), smem, smem, vmem, vmem],
            out_specs=vmem,
            scratch_shapes=scratch,
            compiler_params=pltpu.CompilerParams(
                collective_id=0, has_side_effects=True, vmem_limit_bytes=60 << 20),
            name="graph_layer",
        )(feats, tile_values, source_group.T, live_slots.T, proj_weight, proj_bias.reshape(1, -1))

    return body


def solution(mesh):
    placed = (
        P(("node", "feat"), None),
        P("node", "feat", None, None),
        P("node", "feat"),
        P("node", "feat"),
        P(),
        P(),
    )
    return jax.shard_map(
        make_body(mesh.shape["node"] // 2, mesh.shape["feat"] // 4),
        mesh=mesh, in_specs=placed, out_specs=P(("node", "feat"), None), check_vma=False,
    )
```

```python
import jax
import jax.numpy as jnp
from jax import lax
from jax.experimental import pallas as pl
from jax.experimental.pallas import tpu as pltpu
from jax.sharding import PartitionSpec as P

SLOTS = 3
TOP = 48
LOW = "low"
MESH = pl.DeviceIdType.MESH
HOPS = (
    (0, 0, -1, 0, 0), (0, 1, 0, 0, 0), (0, 0, 2, 0, 0), (1, 1, 0, 0, 0), (0, 1, 1, 0, 0),
    (1, 0, -3, 0, 0), (1, 0, -1, 0, 0), (1, 0, 2, 0, 0), (0, 0, -2, 0, -1), (1, 1, 1, 0, 0),
    (0, 1, -1, 0, -1), (0, 0, 3, 0, 2), (0, 1, -2, 0, -1), (0, 0, 1, 1, 1), (1, 1, -1, 1, 0),
    (0, 1, 2, 1, 1), (1, 1, -3, 0, -3), (1, 0, -4, 0, -3), (1, 0, 3, 0, 2), (1, 0, -2, 0, -1),
    (1, 0, 1, 1, 1), (1, 1, 3, 0, 2), (0, 0, -3, 0, -2), (0, 1, 3, 0, 3), (1, 1, 2, 1, 1),
    (0, 1, -3, 1, -2), (0, 0, 4, 0, 3), (1, 1, -2, 1, -1), (1, 1, -4, 0, -4), (0, 1, 4, 0, 3),
)
F32 = jnp.float32
BF16 = jnp.bfloat16


def make_kernel(ny, nz):
    nodes = 2 * ny
    feats_n = 4 * nz
    half = nz // 2
    last = nz - 1

    def kernel(feats, tiles_hbm, src, live, weight, bias, out,
               tiles, fbuf, own, psend, precv, rsend, rrecv, lsend, lrecv, xsend, xrecv, tsend, trecv,
               dloc, dsend, drecv, dtot, dxrecv,
               tsem, ag_s, ag_r, p_s, p_r, r_s, r_r, l_s, l_r, x_s, x_r, t_s, t_r,
               dr_s, dr_r, dx_s, dx_r):
        n = lax.axis_index("node")
        f = lax.axis_index("feat")
        z = f // 4
        h = (f // 2) % 2
        c = f % 2
        n_x = n + 1 - 2 * (n % 2)
        f_core = f + 1 - 2 * c
        f_opp = f + 2 - 4 * h
        f_up = (f + 4) % feats_n
        f_dn = (f + feats_n - 4) % feats_n
        f_up2 = (f + 8) % feats_n
        f_dn2 = (f + feats_n - 8) % feats_n

        def node_at(x, y):
            return ((n_x if x else n) + nodes + 2 * y) % nodes

        rows_n = tiles_hbm.shape[0]
        parts = tsem.shape[0]
        step_rows = rows_n // parts

        def tile_copy(i):
            sl = pl.ds(i * step_rows, step_rows)
            return pltpu.make_async_copy(tiles_hbm.at[sl], tiles.at[sl], tsem.at[i])

        for i in range(parts):
            tile_copy(i).start()

        barrier = pltpu.get_barrier_semaphore()
        steps = {((x - px) % 2, y - py) for _, x, y, px, py in HOPS}
        steps = sorted(steps | {(x, -y) for x, y in steps})
        near = [(node_at(x, y), f) for x, y in steps]
        near += [(n, fd) for fd in (f_core, f_opp, f_opp + 1 - 2 * c, f_up, f_dn, f_up2, f_dn2)]
        for nd, fd in near:
            pl.semaphore_signal(barrier, inc=1, device_id=dict(node=nd, feat=fd), device_id_type=MESH)
        pl.semaphore_wait(barrier, len(near))

        def remote(s, d, ss, rs, node=None, feat=None):
            dev = dict(node=n if node is None else node, feat=f if feat is None else feat)
            return pltpu.make_async_remote_copy(
                src_ref=s, dst_ref=d, send_sem=ss, recv_sem=rs, device_id=dev, device_id_type=MESH)

        def block_of(x, y):
            return ((n_x if x else n) + nodes - 2 * y) % nodes

        def hop(i):
            q, x, y, px, py = HOPS[i]
            block = block_of(px, py)
            rows = pl.ds(64 * q, 64)
            source = feats.at[rows] if (px, py) == (0, 0) else fbuf.at[block, rows]
            return remote(source, fbuf.at[block, rows], ag_s.at[i], ag_r.at[i], node=node_at((x - px) % 2, y - py))

        def landing(i):
            q, x, y, _, _ = HOPS[i]
            ref = fbuf.at[block_of(x, y), pl.ds(64 * q, 64)]
            return remote(ref, ref, ag_s.at[i], ag_r.at[i], node=n_x)

        def onward(q, x, y):
            for i in range(len(HOPS)):
                if HOPS[i][0] == q and HOPS[i][3:] == (x, y):
                    hop(i).start()

        for i in range(len(HOPS)):
            if HOPS[i][3:] == (0, 0):
                hop(i).start()

        fbuf[n] = feats[...]
        fbuf[nodes] = jnp.zeros_like(feats)
        dloc[...] = jnp.zeros_like(dloc)

        for i in range(len(HOPS)):
            landing(i).wait_recv()
            onward(*HOPS[i][:3])
        for i in range(parts):
            tile_copy(i).wait()

        slot_of = lax.broadcasted_iota(jnp.int32, (16, SLOTS * 128), 1) // 128

        def pair(u):
            return remote(psend.at[u], precv.at[u], p_s.at[u], p_r.at[u], feat=f_core)

        def group(u, j):
            off = jnp.where(u % 2 == 1, half - (u + 1) // 2, half + u // 2)
            zt = (z + off) % nz
            ht = j % 2
            ct = 1 - c if j < 2 else c
            r = 4 * zt + 2 * ht + ct
            count = live[0, r]
            a = jnp.concatenate([tiles[r, s] for s in range(SLOTS)], axis=1)
            b = jnp.concatenate(
                [fbuf[jnp.where(count > s, src[s, r], nodes)] for s in range(SLOTS)], axis=0)
            on = jnp.where(slot_of < count, 1.0, 0.0).astype(BF16)
            got = jnp.dot(a, b, preferred_element_type=F32)
            rowsum = lax.dot_general(on, a, (((1,), (1,)), ((), ())), preferred_element_type=F32)
            dloc[u, pl.ds(2 * ht + ct, 1), :] = rowsum[0:1, :]
            if j < 2:
                psend[u, ht] = got
            else:
                own[u, ht] = got
            if j == 1:
                pair(u).start()

        lanes0 = ((0, 0), (1, 1), (1, 0), (0, 1))
        lanes1 = ((0, LOW), (1, LOW))
        far = ((0, 0), (1, 1), (0, LOW))
        top = slice(0, TOP)
        low = slice(TOP, 128)

        def toward(w, k):
            if k % 2 == 0:
                return f_dn2 if w else f_up2
            return f_dn if w else f_up

        def ring(s, k):
            w, i = s
            if i is LOW:
                return remote(lsend.at[w, k], lrecv.at[w, k], l_s.at[w, k], l_r.at[w, k], feat=toward(w, k))
            return remote(rsend.at[w, i, k], rrecv.at[w, i, k], r_s.at[w, i, k], r_r.at[w, i, k], feat=toward(w, k))

        def dring(w, k):
            return remote(dsend.at[w, k], drecv.at[w, k], dr_s.at[w, k], dr_r.at[w, k], feat=toward(w, k))

        def cross(u):
            return remote(xsend.at[u], xrecv.at[u], x_s.at[u], x_r.at[u], feat=f_opp)

        def both(u, ht, rows):
            return own[u, ht, rows, :] + precv[u, ht, rows, :]

        def unit_of(w, k):
            return 0 if k == 0 else 2 * k - 1 + w

        def arrivals(s, k):
            if k % 2 or k == 0:
                return ()
            return (k - 1, k - 2) if k > 2 or s in far else (k - 1,)

        def arrived(s, k):
            w, i = s
            ring(s, k).wait_recv()
            return (lrecv[w, k] if i is LOW else rrecv[w, i, k]).astype(F32)

        def step(k, active):
            for s in active:
                w, i = s
                u = unit_of(w, k)
                v = both(u, i, top) if i is not LOW else both(u, h, low) + xrecv[u].astype(F32)
                for p in arrivals(s, k):
                    v = v + arrived(s, p)
                if i is not LOW:
                    rsend[w, i, k] = v.astype(BF16)
                else:
                    lsend[w, k] = v.astype(BF16)
                ring(s, k).start()

        def dstep(k):
            for w in range(1 if k == 0 else 2):
                v = dloc[unit_of(w, k)]
                for p in arrivals((0, 0) if w == 0 else (1, 0), k):
                    dring(w, p).wait_recv()
                    v = v + drecv[w, p]
                dsend[w, k] = v
                dring(w, k).start()

        def compute(lo, hi):
            def one(u, carry):
                for j in range(4):
                    group(u, j)
                return carry

            lax.fori_loop(lo, hi, one, 0)

        def send_cross(lo, hi):
            def one(u, carry):
                pair(u).wait_recv()
                xsend[u] = both(u, 1 - h, low).astype(BF16)
                cross(u).start()
                return carry

            lax.fori_loop(lo, hi, one, 0)

        def wait_cross(lo, hi):
            for u in range(lo, hi):
                cross(u).wait_recv()

        e = half - 1
        compute(0, 3)
        send_cross(0, 3)
        step(0, far[:2])
        step(1, lanes0)
        dstep(0)
        dstep(1)
        compute(3, 7)
        send_cross(3, 7)
        step(2, lanes0)
        step(3, lanes0)
        dstep(2)
        dstep(3)
        wait_cross(0, 3)
        step(0, far[2:])
        step(1, lanes1)
        compute(7, nz)
        send_cross(7, nz)
        step(4, lanes0)
        step(5, lanes0)
        dstep(4)
        dstep(5)
        wait_cross(3, 7)
        step(3, lanes1)
        step(2, lanes1)

        def total(i, v):
            for w in range(2):
                for p in (e, e - 1):
                    v = v + arrived((w, i), p)
            return v

        tail = remote(tsend, trecv, t_s, t_r, feat=f_opp)

        def dxc(i):
            return remote(dtot, dxrecv.at[i], dx_s.at[i], dx_r.at[i],
                          feat=(f_core, f_opp, f_opp + 1 - 2 * c)[i])

        tsend[...] = total(1 - h, both(last, 1 - h, top)).astype(BF16)
        tail.start()
        d = dloc[last]
        for w in range(2):
            for p in (e, e - 1):
                dring(w, p).wait_recv()
                d = d + drecv[w, p]
        dtot[...] = d
        for i in range(3):
            dxc(i).start()
        wait_cross(7, nz)
        step(5, lanes1)
        step(4, lanes1)
        kept = total(h, both(last, h, top))
        row = pl.ds(2 * h + c, 1)
        drow = dtot[row, :] + 1.0
        for i in range(3):
            dxc(i).wait_recv()
            drow = drow + dxrecv[i, row, :]
        inv = lax.rsqrt(jnp.broadcast_to(drow, (128, 128)).T)
        inv = jnp.concatenate([inv, inv], axis=1)

        def finish(rows, agg):
            mine = feats[rows, :].astype(F32)
            normed = ((agg + mine) * inv[rows, :]).astype(BF16)
            hidden = jnp.dot(normed, weight[...], preferred_element_type=F32) + bias[...]
            out[rows, :] = (mine + jnp.maximum(hidden, 0.0)).astype(BF16)

        tail.wait_recv()
        finish(top, kept + trecv[...].astype(F32))
        finish(low, total(LOW, both(last, h, low) + xrecv[last].astype(F32)))

        tail.wait_send()
        for i in range(len(HOPS)):
            hop(i).wait_send()
        for i in range(3):
            dxc(i).wait_send()
        def drain(u, carry):
            pair(u).wait_send()
            cross(u).wait_send()
            return carry

        lax.fori_loop(0, nz, drain, 0)

        for k in range(1, half):
            for s in lanes0 + lanes1:
                ring(s, k).wait_send()
            dring(0, k).wait_send()
            dring(1, k).wait_send()
        for s in far:
            ring(s, 0).wait_send()
        dring(0, 0).wait_send()

    return kernel


def make_body(ny, nz):
    nodes = 2 * ny
    half = nz // 2
    dma = pltpu.SemaphoreType.DMA
    vmem = pl.BlockSpec(memory_space=pltpu.VMEM)
    smem = pl.BlockSpec(memory_space=pltpu.SMEM)

    def body(feats, tile_values, source_group, live_slots, proj_weight, proj_bias):
        rows_n = tile_values.shape[0]
        scratch = [
            pltpu.VMEM((rows_n, SLOTS, 128, 128), BF16),
            pltpu.VMEM((nodes + 1, 128, 256), BF16),
            pltpu.VMEM((nz, 2, 128, 256), F32),
            pltpu.VMEM((nz, 2, 128, 256), F32),
            pltpu.VMEM((nz, 2, 128, 256), F32),
            pltpu.VMEM((2, 2, half, TOP, 256), BF16),
            pltpu.VMEM((2, 2, half, TOP, 256), BF16),
            pltpu.VMEM((2, half, 128 - TOP, 256), BF16),
            pltpu.VMEM((2, half, 128 - TOP, 256), BF16),
            pltpu.VMEM((nz, 128 - TOP, 256), BF16),
            pltpu.VMEM((nz, 128 - TOP, 256), BF16),
            pltpu.VMEM((TOP, 256), BF16),
            pltpu.VMEM((TOP, 256), BF16),
            pltpu.VMEM((nz, 8, 128), F32),
            pltpu.VMEM((2, half, 8, 128), F32),
            pltpu.VMEM((2, half, 8, 128), F32),
            pltpu.VMEM((8, 128), F32),
            pltpu.VMEM((3, 8, 128), F32),
            dma((6,)),
            dma((len(HOPS),)), dma((len(HOPS),)),
            dma((nz,)), dma((nz,)),
            dma((2, 2, half)), dma((2, 2, half)),
            dma((2, half)), dma((2, half)),
            dma((nz,)), dma((nz,)),
            dma, dma,
            dma((2, half)), dma((2, half)),
            dma((3,)), dma((3,)),
        ]
        return pl.pallas_call(
            make_kernel(ny, nz),
            out_shape=jax.ShapeDtypeStruct(feats.shape, BF16),
            in_specs=[vmem, pl.BlockSpec(memory_space=pl.ANY), smem, smem, vmem, vmem],
            out_specs=vmem,
            scratch_shapes=scratch,
            compiler_params=pltpu.CompilerParams(
                collective_id=0, has_side_effects=True, vmem_limit_bytes=60 << 20),
            name="graph_layer",
        )(feats, tile_values, source_group.T, live_slots.T, proj_weight, proj_bias.reshape(1, -1))

    return body


def solution(mesh):
    placed = (
        P(("node", "feat"), None),
        P("node", "feat", None, None),
        P("node", "feat"),
        P("node", "feat"),
        P(),
        P(),
    )
    return jax.shard_map(
        make_body(mesh.shape["node"] // 2, mesh.shape["feat"] // 4),
        mesh=mesh, in_specs=placed, out_specs=P(("node", "feat"), None), check_vma=False,
    )
```

```python
import jax
import jax.numpy as jnp
from jax import lax
from jax.experimental import pallas as pl
from jax.experimental.pallas import tpu as pltpu
from jax.sharding import PartitionSpec as P

SLOTS = 3
TOP = 32
LOW = "low"
MESH = pl.DeviceIdType.MESH
HOPS = (
    (0, 0, -1, 0, 0), (0, 1, 0, 0, 0), (0, 0, 2, 0, 0), (1, 1, 0, 0, 0), (0, 1, 1, 0, 0),
    (1, 0, -3, 0, 0), (1, 0, -1, 0, 0), (1, 0, 2, 0, 0), (0, 0, -2, 0, -1), (1, 1, 1, 0, 0),
    (0, 1, -1, 0, -1), (0, 0, 3, 0, 2), (0, 1, -2, 0, -1), (0, 0, 1, 1, 1), (1, 1, -1, 1, 0),
    (0, 1, 2, 1, 1), (1, 1, -3, 0, -3), (1, 0, -4, 0, -3), (1, 0, 3, 0, 2), (1, 0, -2, 0, -1),
    (1, 0, 1, 1, 1), (1, 1, 3, 0, 2), (0, 0, -3, 0, -2), (0, 1, 3, 0, 3), (1, 1, 2, 1, 1),
    (0, 1, -3, 1, -2), (0, 0, 4, 0, 3), (1, 1, -2, 1, -1), (1, 1, -4, 0, -4), (0, 1, 4, 0, 3),
)
F32 = jnp.float32
BF16 = jnp.bfloat16


def make_kernel(ny, nz):
    nodes = 2 * ny
    feats_n = 4 * nz
    half = nz // 2
    last = nz - 1

    def kernel(feats, tiles_hbm, src, live, weight, bias, out,
               tiles, fbuf, own, psend, precv, rsend, rrecv, lsend, lrecv, xsend, xrecv, tsend, trecv,
               dloc, dsend, drecv, dtot, dxrecv,
               tsem, ag_s, ag_r, p_s, p_r, r_s, r_r, l_s, l_r, x_s, x_r, t_s, t_r,
               dr_s, dr_r, dx_s, dx_r):
        n = lax.axis_index("node")
        f = lax.axis_index("feat")
        z = f // 4
        h = (f // 2) % 2
        c = f % 2
        n_x = n + 1 - 2 * (n % 2)
        f_core = f + 1 - 2 * c
        f_opp = f + 2 - 4 * h
        f_up = (f + 4) % feats_n
        f_dn = (f + feats_n - 4) % feats_n
        f_up2 = (f + 8) % feats_n
        f_dn2 = (f + feats_n - 8) % feats_n

        def node_at(x, y):
            return ((n_x if x else n) + nodes + 2 * y) % nodes

        rows_n = tiles_hbm.shape[0]
        parts = tsem.shape[0]
        step_rows = rows_n // parts

        def tile_copy(i):
            sl = pl.ds(i * step_rows, step_rows)
            return pltpu.make_async_copy(tiles_hbm.at[sl], tiles.at[sl], tsem.at[i])

        for i in range(parts):
            tile_copy(i).start()

        barrier = pltpu.get_barrier_semaphore()
        steps = {((x - px) % 2, y - py) for _, x, y, px, py in HOPS}
        steps = sorted(steps | {(x, -y) for x, y in steps})
        near = [(node_at(x, y), f) for x, y in steps]
        near += [(n, fd) for fd in (f_core, f_opp, f_opp + 1 - 2 * c, f_up, f_dn, f_up2, f_dn2)]
        for nd, fd in near:
            pl.semaphore_signal(barrier, inc=1, device_id=dict(node=nd, feat=fd), device_id_type=MESH)
        pl.semaphore_wait(barrier, len(near))

        def remote(s, d, ss, rs, node=None, feat=None):
            dev = dict(node=n if node is None else node, feat=f if feat is None else feat)
            return pltpu.make_async_remote_copy(
                src_ref=s, dst_ref=d, send_sem=ss, recv_sem=rs, device_id=dev, device_id_type=MESH)

        def block_of(x, y):
            return ((n_x if x else n) + nodes - 2 * y) % nodes

        def hop(i):
            q, x, y, px, py = HOPS[i]
            block = block_of(px, py)
            rows = pl.ds(64 * q, 64)
            source = feats.at[rows] if (px, py) == (0, 0) else fbuf.at[block, rows]
            return remote(source, fbuf.at[block, rows], ag_s.at[i], ag_r.at[i], node=node_at((x - px) % 2, y - py))

        def landing(i):
            q, x, y, _, _ = HOPS[i]
            ref = fbuf.at[block_of(x, y), pl.ds(64 * q, 64)]
            return remote(ref, ref, ag_s.at[i], ag_r.at[i], node=n_x)

        def onward(q, x, y):
            for i in range(len(HOPS)):
                if HOPS[i][0] == q and HOPS[i][3:] == (x, y):
                    hop(i).start()

        for i in range(len(HOPS)):
            if HOPS[i][3:] == (0, 0):
                hop(i).start()

        fbuf[n] = feats[...]
        fbuf[nodes] = jnp.zeros_like(feats)
        dloc[...] = jnp.zeros_like(dloc)

        for i in range(len(HOPS)):
            landing(i).wait_recv()
            onward(*HOPS[i][:3])
        for i in range(parts):
            tile_copy(i).wait()

        slot_of = lax.broadcasted_iota(jnp.int32, (16, SLOTS * 128), 1) // 128

        def pair(u):
            return remote(psend.at[u], precv.at[u], p_s.at[u], p_r.at[u], feat=f_core)

        def group(u, j):
            off = jnp.where(u % 2 == 1, half - (u + 1) // 2, half + u // 2)
            zt = (z + off) % nz
            ht = j % 2
            ct = 1 - c if j < 2 else c
            r = 4 * zt + 2 * ht + ct
            count = live[0, r]
            a = jnp.concatenate([tiles[r, s] for s in range(SLOTS)], axis=1)
            b = jnp.concatenate(
                [fbuf[jnp.where(count > s, src[s, r], nodes)] for s in range(SLOTS)], axis=0)
            on = jnp.where(slot_of < count, 1.0, 0.0).astype(BF16)
            got = jnp.dot(a, b, preferred_element_type=F32)
            rowsum = lax.dot_general(on, a, (((1,), (1,)), ((), ())), preferred_element_type=F32)
            dloc[u, pl.ds(2 * ht + ct, 1), :] = rowsum[0:1, :]
            if j < 2:
                psend[u, ht] = got
            else:
                own[u, ht] = got
            if j == 1:
                pair(u).start()

        lanes0 = ((0, 0), (1, 1), (1, 0), (0, 1))
        lanes1 = ((0, LOW), (1, LOW))
        far = ((0, 0), (1, 1), (0, LOW))
        top = slice(0, TOP)
        low = slice(TOP, 128)

        def toward(w, k):
            if k % 2 == 0:
                return f_dn2 if w else f_up2
            return f_dn if w else f_up

        def ring(s, k):
            w, i = s
            if i is LOW:
                return remote(lsend.at[w, k], lrecv.at[w, k], l_s.at[w, k], l_r.at[w, k], feat=toward(w, k))
            return remote(rsend.at[w, i, k], rrecv.at[w, i, k], r_s.at[w, i, k], r_r.at[w, i, k], feat=toward(w, k))

        def dring(w, k):
            return remote(dsend.at[w, k], drecv.at[w, k], dr_s.at[w, k], dr_r.at[w, k], feat=toward(w, k))

        def cross(u):
            return remote(xsend.at[u], xrecv.at[u], x_s.at[u], x_r.at[u], feat=f_opp)

        def both(u, ht, rows):
            return own[u, ht, rows, :] + precv[u, ht, rows, :]

        def unit_of(w, k):
            return 0 if k == 0 else 2 * k - 1 + w

        def arrivals(s, k):
            if k % 2 or k == 0:
                return ()
            return (k - 1, k - 2) if k > 2 or s in far else (k - 1,)

        def arrived(s, k):
            w, i = s
            ring(s, k).wait_recv()
            return (lrecv[w, k] if i is LOW else rrecv[w, i, k]).astype(F32)

        def step(k, active):
            for s in active:
                w, i = s
                u = unit_of(w, k)
                if i is LOW:
                    cross(u).wait_recv()
                    v = both(u, h, low) + xrecv[u].astype(F32)
                else:
                    v = both(u, i, top)
                for p in arrivals(s, k):
                    v = v + arrived(s, p)
                if i is not LOW:
                    rsend[w, i, k] = v.astype(BF16)
                else:
                    lsend[w, k] = v.astype(BF16)
                ring(s, k).start()

        def dstep(k):
            for w in range(1 if k == 0 else 2):
                v = dloc[unit_of(w, k)]
                for p in arrivals((0, 0) if w == 0 else (1, 0), k):
                    dring(w, p).wait_recv()
                    v = v + drecv[w, p]
                dsend[w, k] = v
                dring(w, k).start()

        def compute(lo, hi):
            def one(u, carry):
                for j in range(4):
                    group(u, j)
                return carry

            lax.fori_loop(lo, hi, one, 0)

        def send_cross(lo, hi):
            def one(u, carry):
                pair(u).wait_recv()
                xsend[u] = both(u, 1 - h, low).astype(BF16)
                cross(u).start()
                return carry

            lax.fori_loop(lo, hi, one, 0)

        e = half - 1
        compute(0, 3)
        send_cross(0, 3)
        step(0, far[:2])
        step(1, lanes0)
        dstep(0)
        dstep(1)
        compute(3, 7)
        send_cross(3, 7)
        step(2, lanes0)
        step(3, lanes0)
        dstep(2)
        dstep(3)
        step(0, far[2:])
        step(1, lanes1)
        compute(7, nz)
        send_cross(7, nz)
        step(4, lanes0)
        step(5, lanes0)
        dstep(4)
        dstep(5)
        step(3, lanes1)
        step(2, lanes1)

        def total(i, v):
            for w in range(2):
                for p in (e, e - 1):
                    v = v + arrived((w, i), p)
            return v

        tail = remote(tsend, trecv, t_s, t_r, feat=f_opp)

        def dxc(i):
            return remote(dtot, dxrecv.at[i], dx_s.at[i], dx_r.at[i],
                          feat=(f_core, f_opp, f_opp + 1 - 2 * c)[i])

        tsend[...] = total(1 - h, both(last, 1 - h, top)).astype(BF16)
        tail.start()
        d = dloc[last]
        for w in range(2):
            for p in (e, e - 1):
                dring(w, p).wait_recv()
                d = d + drecv[w, p]
        dtot[...] = d
        for i in range(3):
            dxc(i).start()
        step(5, lanes1)
        step(4, lanes1)
        kept = total(h, both(last, h, top))
        row = pl.ds(2 * h + c, 1)
        drow = dtot[row, :] + 1.0
        for i in range(3):
            dxc(i).wait_recv()
            drow = drow + dxrecv[i, row, :]
        inv = lax.rsqrt(jnp.broadcast_to(drow, (128, 128)).T)
        inv = jnp.concatenate([inv, inv], axis=1)

        def finish(rows, agg):
            mine = feats[rows, :].astype(F32)
            normed = ((agg + mine) * inv[rows, :]).astype(BF16)
            hidden = jnp.dot(normed, weight[...], preferred_element_type=F32) + bias[...]
            out[rows, :] = (mine + jnp.maximum(hidden, 0.0)).astype(BF16)

        tail.wait_recv()
        finish(top, kept + trecv[...].astype(F32))
        cross(last).wait_recv()
        finish(low, total(LOW, both(last, h, low) + xrecv[last].astype(F32)))

        tail.wait_send()
        for i in range(len(HOPS)):
            hop(i).wait_send()
        for i in range(3):
            dxc(i).wait_send()
        def drain(u, carry):
            pair(u).wait_send()
            cross(u).wait_send()
            return carry

        lax.fori_loop(0, nz, drain, 0)

        for k in range(1, half):
            for s in lanes0 + lanes1:
                ring(s, k).wait_send()
            dring(0, k).wait_send()
            dring(1, k).wait_send()
        for s in far:
            ring(s, 0).wait_send()
        dring(0, 0).wait_send()

    return kernel


def make_body(ny, nz):
    nodes = 2 * ny
    half = nz // 2
    dma = pltpu.SemaphoreType.DMA
    vmem = pl.BlockSpec(memory_space=pltpu.VMEM)
    smem = pl.BlockSpec(memory_space=pltpu.SMEM)

    def body(feats, tile_values, source_group, live_slots, proj_weight, proj_bias):
        rows_n = tile_values.shape[0]
        scratch = [
            pltpu.VMEM((rows_n, SLOTS, 128, 128), BF16),
            pltpu.VMEM((nodes + 1, 128, 256), BF16),
            pltpu.VMEM((nz, 2, 128, 256), F32),
            pltpu.VMEM((nz, 2, 128, 256), F32),
            pltpu.VMEM((nz, 2, 128, 256), F32),
            pltpu.VMEM((2, 2, half, TOP, 256), BF16),
            pltpu.VMEM((2, 2, half, TOP, 256), BF16),
            pltpu.VMEM((2, half, 128 - TOP, 256), BF16),
            pltpu.VMEM((2, half, 128 - TOP, 256), BF16),
            pltpu.VMEM((nz, 128 - TOP, 256), BF16),
            pltpu.VMEM((nz, 128 - TOP, 256), BF16),
            pltpu.VMEM((TOP, 256), BF16),
            pltpu.VMEM((TOP, 256), BF16),
            pltpu.VMEM((nz, 8, 128), F32),
            pltpu.VMEM((2, half, 8, 128), F32),
            pltpu.VMEM((2, half, 8, 128), F32),
            pltpu.VMEM((8, 128), F32),
            pltpu.VMEM((3, 8, 128), F32),
            dma((6,)),
            dma((len(HOPS),)), dma((len(HOPS),)),
            dma((nz,)), dma((nz,)),
            dma((2, 2, half)), dma((2, 2, half)),
            dma((2, half)), dma((2, half)),
            dma((nz,)), dma((nz,)),
            dma, dma,
            dma((2, half)), dma((2, half)),
            dma((3,)), dma((3,)),
        ]
        return pl.pallas_call(
            make_kernel(ny, nz),
            out_shape=jax.ShapeDtypeStruct(feats.shape, BF16),
            in_specs=[vmem, pl.BlockSpec(memory_space=pl.ANY), smem, smem, vmem, vmem],
            out_specs=vmem,
            scratch_shapes=scratch,
            compiler_params=pltpu.CompilerParams(
                collective_id=0, has_side_effects=True, vmem_limit_bytes=60 << 20),
            name="graph_layer",
        )(feats, tile_values, source_group.T, live_slots.T, proj_weight, proj_bias.reshape(1, -1))

    return body


def solution(mesh):
    placed = (
        P(("node", "feat"), None),
        P("node", "feat", None, None),
        P("node", "feat"),
        P("node", "feat"),
        P(),
        P(),
    )
    return jax.shard_map(
        make_body(mesh.shape["node"] // 2, mesh.shape["feat"] // 4),
        mesh=mesh, in_specs=placed, out_specs=P(("node", "feat"), None), check_vma=False,
    )
```

```python
import jax
import jax.numpy as jnp
from jax import lax
from jax.experimental import pallas as pl
from jax.experimental.pallas import tpu as pltpu
from jax.sharding import PartitionSpec as P

SLOTS = 3
TOP = 32
LOW = "low"
MESH = pl.DeviceIdType.MESH
HOPS = (
    (0, 0, -1, 0, 0), (0, 1, 0, 0, 0), (0, 0, 2, 0, 0), (1, 1, 0, 0, 0), (0, 1, 1, 0, 0),
    (1, 0, -3, 0, 0), (1, 0, -1, 0, 0), (1, 0, 2, 0, 0), (0, 0, -2, 0, -1), (1, 1, 1, 0, 0),
    (0, 1, -1, 0, -1), (0, 0, 3, 0, 2), (0, 1, -2, 0, -1), (0, 0, 1, 1, 1), (1, 1, -1, 1, 0),
    (0, 1, 2, 1, 1), (1, 1, -3, 0, -3), (1, 0, -4, 0, -3), (1, 0, 3, 0, 2), (1, 0, -2, 0, -1),
    (1, 0, 1, 1, 1), (1, 1, 3, 0, 2), (0, 0, -3, 0, -2), (0, 1, 3, 0, 3), (1, 1, 2, 1, 1),
    (0, 1, -3, 1, -2), (0, 0, 4, 0, 3), (1, 1, -2, 1, -1), (1, 1, -4, 0, -4), (0, 1, 4, 0, 3),
)
F32 = jnp.float32
BF16 = jnp.bfloat16


def make_kernel(ny, nz):
    nodes = 2 * ny
    feats_n = 4 * nz
    half = nz // 2
    last = nz - 1

    def kernel(feats, tiles_hbm, src, live, weight, bias, out,
               tiles, fbuf, own, psend, precv, rsend, rrecv, lsend, lrecv, xsend, xrecv, tsend, trecv,
               dloc, dsend, drecv, dtot, dxrecv,
               tsem, ag_s, ag_r, p_s, p_r, r_s, r_r, l_s, l_r, x_s, x_r, t_s, t_r,
               dr_s, dr_r, dx_s, dx_r):
        n = lax.axis_index("node")
        f = lax.axis_index("feat")
        z = f // 4
        h = (f // 2) % 2
        c = f % 2
        n_x = n + 1 - 2 * (n % 2)
        f_core = f + 1 - 2 * c
        f_opp = f + 2 - 4 * h
        f_up = (f + 4) % feats_n
        f_dn = (f + feats_n - 4) % feats_n
        f_up2 = (f + 8) % feats_n
        f_dn2 = (f + feats_n - 8) % feats_n

        def node_at(x, y):
            return ((n_x if x else n) + nodes + 2 * y) % nodes

        rows_n = tiles_hbm.shape[0]
        parts = tsem.shape[0]
        step_rows = rows_n // parts

        def tile_copy(i):
            sl = pl.ds(i * step_rows, step_rows)
            return pltpu.make_async_copy(tiles_hbm.at[sl], tiles.at[sl], tsem.at[i])

        for i in range(parts):
            tile_copy(i).start()

        barrier = pltpu.get_barrier_semaphore()
        steps = {((x - px) % 2, y - py) for _, x, y, px, py in HOPS}
        steps = sorted(steps | {(x, -y) for x, y in steps})
        near = [(node_at(x, y), f) for x, y in steps]
        near += [(n, fd) for fd in (f_core, f_opp, f_opp + 1 - 2 * c, f_up, f_dn, f_up2, f_dn2)]
        for nd, fd in near:
            pl.semaphore_signal(barrier, inc=1, device_id=dict(node=nd, feat=fd), device_id_type=MESH)
        pl.semaphore_wait(barrier, len(near))

        def remote(s, d, ss, rs, node=None, feat=None):
            dev = dict(node=n if node is None else node, feat=f if feat is None else feat)
            return pltpu.make_async_remote_copy(
                src_ref=s, dst_ref=d, send_sem=ss, recv_sem=rs, device_id=dev, device_id_type=MESH)

        def block_of(x, y):
            return ((n_x if x else n) + nodes - 2 * y) % nodes

        def hop(i):
            q, x, y, px, py = HOPS[i]
            block = block_of(px, py)
            rows = pl.ds(64 * q, 64)
            source = feats.at[rows] if (px, py) == (0, 0) else fbuf.at[block, rows]
            return remote(source, fbuf.at[block, rows], ag_s.at[i], ag_r.at[i], node=node_at((x - px) % 2, y - py))

        def landing(i):
            q, x, y, _, _ = HOPS[i]
            ref = fbuf.at[block_of(x, y), pl.ds(64 * q, 64)]
            return remote(ref, ref, ag_s.at[i], ag_r.at[i], node=n_x)

        def onward(q, x, y):
            for i in range(len(HOPS)):
                if HOPS[i][0] == q and HOPS[i][3:] == (x, y):
                    hop(i).start()

        for i in range(len(HOPS)):
            if HOPS[i][3:] == (0, 0):
                hop(i).start()

        fbuf[n] = feats[...]
        fbuf[nodes] = jnp.zeros_like(feats)
        dloc[...] = jnp.zeros_like(dloc)

        for i in range(len(HOPS)):
            landing(i).wait_recv()
            onward(*HOPS[i][:3])
        for i in range(parts):
            tile_copy(i).wait()

        slot_of = lax.broadcasted_iota(jnp.int32, (16, SLOTS * 128), 1) // 128

        def pair(u):
            return remote(psend.at[u], precv.at[u], p_s.at[u], p_r.at[u], feat=f_core)

        def group(u, j):
            off = jnp.where(u % 2 == 1, half - (u + 1) // 2, half + u // 2)
            zt = (z + off) % nz
            ht = j % 2
            ct = 1 - c if j < 2 else c
            r = 4 * zt + 2 * ht + ct
            count = live[0, r]
            a = jnp.concatenate([tiles[r, s] for s in range(SLOTS)], axis=1)
            b = jnp.concatenate(
                [fbuf[jnp.where(count > s, src[s, r], nodes)] for s in range(SLOTS)], axis=0)
            on = jnp.where(slot_of < count, 1.0, 0.0).astype(BF16)
            got = jnp.dot(a, b, preferred_element_type=F32)
            rowsum = lax.dot_general(on, a, (((1,), (1,)), ((), ())), preferred_element_type=F32)
            dloc[u, pl.ds(2 * ht + ct, 1), :] = rowsum[0:1, :]
            if j < 2:
                psend[u, ht] = got
            else:
                own[u, ht] = got
            if j == 1:
                pair(u).start()

        lanes0 = ((0, 0), (1, 1), (1, 0), (0, 1))
        lanes1 = ((0, LOW), (1, LOW))
        far = ((0, 0), (1, 1), (0, LOW))
        top = slice(0, TOP)
        low = slice(TOP, 128)

        def toward(w, k):
            if k % 2 == 0:
                return f_dn2 if w else f_up2
            return f_dn if w else f_up

        def ring(s, k):
            w, i = s
            if i is LOW:
                return remote(lsend.at[w, k], lrecv.at[w, k], l_s.at[w, k], l_r.at[w, k], feat=toward(w, k))
            return remote(rsend.at[w, i, k], rrecv.at[w, i, k], r_s.at[w, i, k], r_r.at[w, i, k], feat=toward(w, k))

        def dring(w, k):
            return remote(dsend.at[w, k], drecv.at[w, k], dr_s.at[w, k], dr_r.at[w, k], feat=toward(w, k))

        def cross(u):
            return remote(xsend.at[u], xrecv.at[u], x_s.at[u], x_r.at[u], feat=f_opp)

        def both(u, ht, rows):
            return own[u, ht, rows, :] + precv[u, ht, rows, :]

        def unit_of(w, k):
            return 0 if k == 0 else 2 * k - 1 + w

        def arrivals(s, k):
            if k % 2 or k == 0:
                return ()
            return (k - 1, k - 2) if k > 2 or s in far else (k - 1,)

        def arrived(s, k):
            w, i = s
            ring(s, k).wait_recv()
            return (lrecv[w, k] if i is LOW else rrecv[w, i, k]).astype(F32)

        def step(k, active):
            for s in active:
                w, i = s
                u = unit_of(w, k)
                if i is LOW:
                    cross(u).wait_recv()
                    v = both(u, h, low) + xrecv[u].astype(F32)
                else:
                    v = both(u, i, top)
                for p in arrivals(s, k):
                    v = v + arrived(s, p)
                if i is not LOW:
                    rsend[w, i, k] = v.astype(BF16)
                else:
                    lsend[w, k] = v.astype(BF16)
                ring(s, k).start()

        def dstep(k):
            for w in range(1 if k == 0 else 2):
                v = dloc[unit_of(w, k)]
                for p in arrivals((0, 0) if w == 0 else (1, 0), k):
                    dring(w, p).wait_recv()
                    v = v + drecv[w, p]
                dsend[w, k] = v
                dring(w, k).start()

        def compute(lo, hi):
            def one(u, carry):
                for j in range(4):
                    group(u, j)
                return carry

            lax.fori_loop(lo, hi, one, 0)

        def send_cross(lo, hi):
            def one(u, carry):
                pair(u).wait_recv()
                xsend[u] = both(u, 1 - h, low).astype(BF16)
                cross(u).start()
                return carry

            lax.fori_loop(lo, hi, one, 0)

        e = half - 1
        compute(0, 3)
        send_cross(0, 3)
        step(0, far[:2])
        step(1, lanes0)
        dstep(0)
        dstep(1)
        compute(3, 7)
        send_cross(3, 7)
        dstep(3)
        step(2, lanes0)
        step(3, lanes0)
        dstep(2)
        step(0, far[2:])
        step(1, lanes1)
        compute(7, nz)
        send_cross(7, nz)
        dstep(5)
        step(4, lanes0)
        dstep(4)
        step(5, lanes0)
        step(3, lanes1)
        step(2, lanes1)

        def total(i, v):
            for w in range(2):
                for p in (e, e - 1):
                    v = v + arrived((w, i), p)
            return v

        tail = remote(tsend, trecv, t_s, t_r, feat=f_opp)

        def dxc(i):
            return remote(dtot, dxrecv.at[i], dx_s.at[i], dx_r.at[i],
                          feat=(f_core, f_opp, f_opp + 1 - 2 * c)[i])

        d = dloc[last]
        for w in range(2):
            for p in (e, e - 1):
                dring(w, p).wait_recv()
                d = d + drecv[w, p]
        dtot[...] = d
        for i in range(3):
            dxc(i).start()
        tsend[...] = total(1 - h, both(last, 1 - h, top)).astype(BF16)
        tail.start()
        step(5, lanes1)
        step(4, lanes1)
        kept = total(h, both(last, h, top))
        row = pl.ds(2 * h + c, 1)
        drow = dtot[row, :] + 1.0
        for i in range(3):
            dxc(i).wait_recv()
            drow = drow + dxrecv[i, row, :]
        inv = lax.rsqrt(jnp.broadcast_to(drow, (128, 128)).T)
        inv = jnp.concatenate([inv, inv], axis=1)

        def finish(rows, agg):
            mine = feats[rows, :].astype(F32)
            normed = ((agg + mine) * inv[rows, :]).astype(BF16)
            hidden = jnp.dot(normed, weight[...], preferred_element_type=F32) + bias[...]
            out[rows, :] = (mine + jnp.maximum(hidden, 0.0)).astype(BF16)

        tail.wait_recv()
        finish(top, kept + trecv[...].astype(F32))
        cross(last).wait_recv()
        finish(low, total(LOW, both(last, h, low) + xrecv[last].astype(F32)))

        tail.wait_send()
        for i in range(len(HOPS)):
            hop(i).wait_send()
        for i in range(3):
            dxc(i).wait_send()
        def drain(u, carry):
            pair(u).wait_send()
            cross(u).wait_send()
            return carry

        lax.fori_loop(0, nz, drain, 0)

        for k in range(1, half):
            for s in lanes0 + lanes1:
                ring(s, k).wait_send()
            dring(0, k).wait_send()
            dring(1, k).wait_send()
        for s in far:
            ring(s, 0).wait_send()
        dring(0, 0).wait_send()

    return kernel


def make_body(ny, nz):
    nodes = 2 * ny
    half = nz // 2
    dma = pltpu.SemaphoreType.DMA
    vmem = pl.BlockSpec(memory_space=pltpu.VMEM)
    smem = pl.BlockSpec(memory_space=pltpu.SMEM)

    def body(feats, tile_values, source_group, live_slots, proj_weight, proj_bias):
        rows_n = tile_values.shape[0]
        scratch = [
            pltpu.VMEM((rows_n, SLOTS, 128, 128), BF16),
            pltpu.VMEM((nodes + 1, 128, 256), BF16),
            pltpu.VMEM((nz, 2, 128, 256), F32),
            pltpu.VMEM((nz, 2, 128, 256), F32),
            pltpu.VMEM((nz, 2, 128, 256), F32),
            pltpu.VMEM((2, 2, half, TOP, 256), BF16),
            pltpu.VMEM((2, 2, half, TOP, 256), BF16),
            pltpu.VMEM((2, half, 128 - TOP, 256), BF16),
            pltpu.VMEM((2, half, 128 - TOP, 256), BF16),
            pltpu.VMEM((nz, 128 - TOP, 256), BF16),
            pltpu.VMEM((nz, 128 - TOP, 256), BF16),
            pltpu.VMEM((TOP, 256), BF16),
            pltpu.VMEM((TOP, 256), BF16),
            pltpu.VMEM((nz, 8, 128), F32),
            pltpu.VMEM((2, half, 8, 128), F32),
            pltpu.VMEM((2, half, 8, 128), F32),
            pltpu.VMEM((8, 128), F32),
            pltpu.VMEM((3, 8, 128), F32),
            dma((6,)),
            dma((len(HOPS),)), dma((len(HOPS),)),
            dma((nz,)), dma((nz,)),
            dma((2, 2, half)), dma((2, 2, half)),
            dma((2, half)), dma((2, half)),
            dma((nz,)), dma((nz,)),
            dma, dma,
            dma((2, half)), dma((2, half)),
            dma((3,)), dma((3,)),
        ]
        return pl.pallas_call(
            make_kernel(ny, nz),
            out_shape=jax.ShapeDtypeStruct(feats.shape, BF16),
            in_specs=[vmem, pl.BlockSpec(memory_space=pl.ANY), smem, smem, vmem, vmem],
            out_specs=vmem,
            scratch_shapes=scratch,
            compiler_params=pltpu.CompilerParams(
                collective_id=0, has_side_effects=True, vmem_limit_bytes=60 << 20),
            name="graph_layer",
        )(feats, tile_values, source_group.T, live_slots.T, proj_weight, proj_bias.reshape(1, -1))

    return body


def solution(mesh):
    placed = (
        P(("node", "feat"), None),
        P("node", "feat", None, None),
        P("node", "feat"),
        P("node", "feat"),
        P(),
        P(),
    )
    return jax.shard_map(
        make_body(mesh.shape["node"] // 2, mesh.shape["feat"] // 4),
        mesh=mesh, in_specs=placed, out_specs=P(("node", "feat"), None), check_vma=False,
    )
```
